32 devices in a mesh: lon: 16 (over z, x, core), lev: 2 (over y).
Axes of the slice: x: 2, y: 2, z: 4, core: 2. Of those that a mesh axis runs over, the one named last changes fastest.
Arguments:
- cotangent: float32 [5, 8, 2880, 1024], P(None, 'lev', 'lon'), may hold values from -6 to 6
- zonal_coef: float32 [8, 2880, 1024], P('lev', 'lon'), may hold values from -0.5 to 0.5
- merid_coef: float32 [8, 2880, 1024], P('lev', 'lon'), may hold values from -0.5 to 0.5
- vertical_wind: float32 [8, 2880, 1024], P('lev', 'lon'), may hold values from -0.5 to 0.5
- cutoff: int32 [64], replicated, may hold values from 1 to 360, as said below
Outputs:
- adjoint_state: float32 [5, 8, 2880, 1024], P(None, 'lev', 'lon')
The draws below stay inside these ranges and needn't reach their ends.
Inputs may be any that keep to these rules, and one draw needn't show every extreme that they name: Every draw holds a row with cutoff exactly 360 and a row with cutoff exactly 1.
All inputs are finite; a program needn't handle non-finite values.
Results may differ from the reference program's by a relative error of at most 0.00023.
Values sent between devices are 32-bit elements; how exact they have to be, the bound alone decides.
A program may use at most 192 MiB of HBM per device.

```python
import jax
import jax.numpy as jnp

NLON = 2880
NLEV = 8
NLAT = 1024
POLAR = 32
KMAX = 360


def draw_cutoff(key, part):
    first_key, second_key, third_key = jax.random.split(jax.random.fold_in(key, 17), 3)
    values = jax.random.randint(first_key, (2 * POLAR,), 1, KMAX + 1)
    position = jax.random.randint(second_key, (), 0, 2 * POLAR)
    offset = jax.random.randint(third_key, (), 1, 2 * POLAR)
    values = values.at[position].set(KMAX)
    values = values.at[(position + offset) % (2 * POLAR)].set(1)
    return values.astype(jnp.int32)


def level_of(stream_key, shape, shards, smallest, high):
    level = 1.0
    for axis_at, parts in shards:
        heights = jax.random.uniform(jax.random.fold_in(jax.random.fold_in(stream_key, 6), axis_at), (parts,), jnp.float32, smallest / len(shards), high / len(shards))
        level = level * jnp.repeat(jnp.exp(heights), shape[axis_at] // parts).reshape((-1,) + (1,) * (len(shape) - 1 - axis_at))
    return level


def normal_values(rng, extent, width, bound, cuts=(), kind=jnp.bfloat16):
    loudness = level_of(rng, extent, cuts, -0.22, 0.18) if cuts else 1.0
    entries = jax.random.normal(rng, extent, jnp.float32) * width * loudness
    return jnp.minimum(jnp.maximum(entries, -bound), bound).astype(kind)


def setup_inputs(seed: int = 0) -> dict:
    key_of = jax.random.split(jax.random.key(seed), 6)
    return {
        "cotangent": normal_values(key_of[0], (5, NLEV, NLON, NLAT), 1.0, 6.0, ((1, 2), (2, 16)), jnp.float32),
        "zonal_coef": jnp.clip(jax.random.uniform(key_of[1], (NLEV, NLON, NLAT), jnp.float32, -0.5, 0.5) * level_of(key_of[1], (NLEV, NLON, NLAT), ((0, 2), (1, 16)), -0.4, 0.0), -0.5, 0.5),
        "merid_coef": jnp.clip(jax.random.uniform(key_of[2], (NLEV, NLON, NLAT), jnp.float32, -0.5, 0.5) * level_of(key_of[2], (NLEV, NLON, NLAT), ((0, 2), (1, 16)), -0.4, 0.0), -0.5, 0.5),
        "vertical_wind": jnp.clip(jax.random.uniform(key_of[3], (NLEV, NLON, NLAT), jnp.float32, -0.5, 0.5) * level_of(key_of[3], (NLEV, NLON, NLAT), ((0, 2), (1, 16)), -0.4, 0.0), -0.5, 0.5),
        "cutoff": draw_cutoff(jax.random.fold_in(key_of[5], 71), 0),
    }


COUPLE_G = 0.3
COUPLE_H = 0.3
COUPLE_B = 0.2


def diff_lon(field):
    return jnp.roll(field, -1, axis=2) - jnp.roll(field, 1, axis=2)


def diff_lat(field):
    padded = jnp.pad(field, ((0, 0), (0, 0), (0, 0), (1, 1)))
    return padded[..., 2:] - padded[..., :-2]


def reference(cotangent, zonal_coef, merid_coef, vertical_wind, cutoff):
    weighted = vertical_wind[None] * cotangent
    padded = jnp.pad(weighted, ((0, 0), (1, 1), (0, 0), (0, 0)))
    adjoint_one = cotangent + (padded[:, 2:] - padded[:, :-2])
    below_sums = jnp.flip(jnp.cumsum(jnp.flip(cotangent[2], 0), 0), 0)
    adjoint_one = adjoint_one.at[3].add(-COUPLE_B * below_sums)
    polar_rows = jnp.concatenate([adjoint_one[..., :POLAR], adjoint_one[..., NLAT - POLAR:]], axis=3)
    spectrum = jnp.fft.rfft(polar_rows, axis=2)
    wavenum = jnp.arange(NLON // 2 + 1, dtype=jnp.int32)[:, None]
    keep_mask = wavenum <= cutoff[None, :]
    spectrum = jnp.where(keep_mask[None, None], spectrum, 0.0)
    smoothed = jnp.fft.irfft(spectrum, n=NLON, axis=2).astype(adjoint_one.dtype)
    filtered = jnp.concatenate([smoothed[..., :POLAR], adjoint_one[..., POLAR:NLAT - POLAR], smoothed[..., POLAR:]], axis=3)
    zonal_part = zonal_coef[None] * filtered
    zonal_flux = jnp.stack([zonal_part[0] + COUPLE_H * filtered[3], zonal_part[1], zonal_part[2], zonal_part[3] + COUPLE_G * filtered[0], zonal_part[4]])
    merid_part = merid_coef[None] * filtered
    merid_flux = jnp.stack([merid_part[0], merid_part[1] + COUPLE_H * filtered[3], merid_part[2], merid_part[3] + COUPLE_G * filtered[1], merid_part[4]])
    return adjoint_one + diff_lon(zonal_flux) + diff_lat(merid_flux)
```

```python
import functools
import math

import jax
import jax.numpy as jnp
from jax import lax
from jax.experimental import pallas as pl
from jax.experimental.pallas import tpu as pltpu
from jax.sharding import PartitionSpec as P

POLAR = 32
KMAX = 360
COUPLE_G = 0.3
COUPLE_H = 0.3
COUPLE_B = 0.2
WIDE = 256
MESH = pl.DeviceIdType.MESH
HIGHEST = lax.Precision.HIGHEST


def angles(left, right, period):
    turn = (left * right) % period
    phase = turn.astype(jnp.float32) * (2.0 * math.pi / period)
    return jnp.cos(phase), jnp.sin(phase)


def filter_kernel(
    peers, x_ref, fwd_ref, inv_ref, ct_ref, st_ref, mask_ref, out_ref, held, made,
    own_sem, send_a, recv_a, send_b, recv_b,
):
    me = lax.axis_index("lon")
    kpad = ct_ref.shape[2]
    barrier = pltpu.get_barrier_semaphore()

    def greet(o, _):
        pl.semaphore_signal(
            barrier, inc=1, device_id={"lon": lax.rem(me + o, peers)}, device_id_type=MESH
        )
        return 0

    lax.fori_loop(1, peers, greet, 0)
    pl.semaphore_wait(barrier, peers - 1)

    def out_copy(o):
        d = lax.rem(me + o, peers)
        return pltpu.make_async_remote_copy(
            src_ref=x_ref.at[d], dst_ref=held.at[me], send_sem=send_a.at[d],
            recv_sem=recv_a.at[me], device_id={"lon": d}, device_id_type=MESH,
        )

    def in_copy(o):
        s = lax.rem(me + o, peers)
        return pltpu.make_async_remote_copy(
            src_ref=x_ref.at[s], dst_ref=held.at[s], send_sem=send_a.at[s],
            recv_sem=recv_a.at[s], device_id={"lon": s}, device_id_type=MESH,
        )

    def back_copy(o):
        d = lax.rem(me + o, peers)
        return pltpu.make_async_remote_copy(
            src_ref=made.at[d], dst_ref=out_ref.at[me], send_sem=send_b.at[d],
            recv_sem=recv_b.at[me], device_id={"lon": d}, device_id_type=MESH,
        )

    def home_copy(o):
        s = lax.rem(me + o, peers)
        return pltpu.make_async_remote_copy(
            src_ref=made.at[s], dst_ref=out_ref.at[s], send_sem=send_b.at[s],
            recv_sem=recv_b.at[s], device_id={"lon": s}, device_id_type=MESH,
        )

    lax.fori_loop(1, peers, lambda o, c: (out_copy(o).start(), c)[1], 0)
    own = pltpu.make_async_copy(x_ref.at[me], held.at[me], own_sem)
    own.start()
    own.wait()
    lax.fori_loop(1, peers, lambda o, c: (in_copy(o).wait_recv(), c)[1], 0)

    cols = held.shape[1]
    zero = jnp.zeros((cols, kpad), jnp.float32)

    def gather(s, carry):
        a, b = carry
        both = jnp.dot(held[s], fwd_ref[...], precision=HIGHEST, preferred_element_type=jnp.float32)
        c, v = both[:, :kpad], both[:, kpad:]
        ct, st = ct_ref[s], st_ref[s]
        return a + (ct * c - st * v), b + (st * c + ct * v)

    a, b = lax.fori_loop(0, peers, gather, (zero, zero))
    a = a * mask_ref[...]
    b = b * mask_ref[...]

    def spread(d, carry):
        a, b = carry
        ct, st = ct_ref[d], st_ref[d]
        made[d] = jnp.dot(
            a * ct + b * st, inv_ref[0], precision=HIGHEST, preferred_element_type=jnp.float32
        ) + jnp.dot(
            b * ct - a * st, inv_ref[1], precision=HIGHEST, preferred_element_type=jnp.float32
        )
        return carry

    lax.fori_loop(0, peers, spread, (a, b))
    lax.fori_loop(1, peers, lambda o, c: (back_copy(o).start(), c)[1], 0)
    mine = pltpu.make_async_copy(made.at[me], out_ref.at[me], own_sem)
    mine.start()
    mine.wait()
    lax.fori_loop(1, peers, lambda o, c: (home_copy(o).wait_recv(), c)[1], 0)
    lax.fori_loop(1, peers, lambda o, c: (out_copy(o).wait_send(), c)[1], 0)
    lax.fori_loop(1, peers, lambda o, c: (back_copy(o).wait_send(), c)[1], 0)


def polar_filter(x, cutoff, peers):
    _, cols, lon_dev = x.shape
    nlon = peers * lon_dev
    rows = cutoff.shape[0] // peers
    kpad = (KMAX + 1 + 127) // 128 * 128
    wave = jnp.arange(kpad, dtype=jnp.int32)
    place = jnp.arange(lon_dev, dtype=jnp.int32)
    fwd = jnp.concatenate(angles(place[:, None], wave[None, :], nlon), axis=1)
    wide = jnp.arange(-1, lon_dev + 1, dtype=jnp.int32)
    inv = jnp.stack(angles(wave[:, None], wide[None, :] % nlon, nlon))
    seat = jnp.arange(peers, dtype=jnp.int32) * lon_dev
    ct, st = angles(seat[:, None, None], wave[None, None, :], nlon)
    mine = lax.dynamic_slice_in_dim(cutoff, lax.axis_index("lon") * rows, rows)
    weight = jnp.where(wave == 0, 1.0 / nlon, 2.0 / nlon)
    mask = jnp.where(wave[None, :] <= mine[:, None], weight[None, :], 0.0)
    mask = jnp.tile(mask, (cols // rows, 1))
    vmem = pl.BlockSpec(memory_space=pltpu.VMEM)
    dma = pltpu.SemaphoreType.DMA
    return pl.pallas_call(
        functools.partial(filter_kernel, peers),
        out_shape=jax.ShapeDtypeStruct((peers, cols, lon_dev + 2), jnp.float32),
        in_specs=[vmem] * 6,
        out_specs=vmem,
        scratch_shapes=[
            pltpu.VMEM((peers, cols, lon_dev), jnp.float32),
            pltpu.VMEM((peers, cols, lon_dev + 2), jnp.float32),
            dma(()), dma((peers,)), dma((peers,)), dma((peers,)), dma((peers,)),
        ],
        compiler_params=pltpu.CompilerParams(
            collective_id=0, has_side_effects=True, vmem_limit_bytes=24 << 20
        ),
        cost_estimate=pl.CostEstimate(flops=8_000_000_000, bytes_accessed=60_000_000, transcendentals=0),
        name="polar_filter",
    )(x, fwd, inv, ct, st, mask)


def coupled(coef, fields, first):
    flux = [coef * f for f in fields]
    flux[first] = flux[first] + COUPLE_H * fields[3]
    flux[3] = flux[3] + COUPLE_G * fields[first]
    return flux


def stencil_kernel(tiles, levels, n_edge, n_old, ids, flags, cot, vw, zc, mc, tail, smooth, halo, *rest):
    edges = rest[:n_edge]
    out, filt, done, rim = rest[n_edge + n_old :]
    t, i = pl.program_id(0), pl.program_id(1)
    k = ids[i]
    width = filt.shape[2]
    lon = filt.shape[1]

    @pl.when(t < tiles)
    def _():
        upper = jnp.minimum(k + 1, levels - 1)
        lower = jnp.maximum(k - 1, 0)
        wind_up = vw[upper] * flags[0, i]
        wind_dn = vw[lower] * flags[1, i]
        base = []
        for f in range(5):
            a = cot[f, k] + (wind_up * cot[f, upper] - wind_dn * cot[f, lower])
            for n, e in enumerate(edges):
                a = a + flags[2 + n, i] * e[f]
            if f == 3:
                below = tail[...]
                for m in range(levels):
                    below = below + jnp.where(m >= k, 1.0, 0.0) * cot[2, m]
                a = a - COUPLE_B * below
            base.append(a)
            filt[f] = a
        lane = lax.broadcasted_iota(jnp.int32, (lon, 128), 1)

        @pl.when(t == 0)
        def _():
            for f in range(5):
                filt[f, :, :128] = jnp.where(lane < POLAR, smooth[f, 0], filt[f, :, :128])

        @pl.when(t == tiles - 1)
        def _():
            for f in range(5):
                filt[f, :, width - 128 :] = jnp.where(
                    lane >= 128 - POLAR, smooth[f, 0], filt[f, :, width - 128 :]
                )

        fields = [filt[f] for f in range(5)]
        zonal = coupled(zc[0], fields, 0)
        merid = coupled(mc[0], fields, 1)
        place = lax.broadcasted_iota(jnp.int32, (lon, width), 1)
        for f in range(5):
            ahead = jnp.concatenate([zonal[f][1:], halo[f, 0, 1:2]], 0)
            behind = jnp.concatenate([halo[f, 0, 0:1], zonal[f][:-1]], 0)
            total = base[f] + (ahead - behind)
            right = jnp.concatenate([merid[f][:, 1:], merid[f][:, :1]], 1)
            left = jnp.concatenate([merid[f][:, width - 1 :], merid[f][:, : width - 1]], 1)
            out[f, 0] = done[i, f] + jnp.where(place == width - 1, right, 0.0)
            total = total + jnp.where(place == width - 1, 0.0, right)
            edge = jnp.where(t > 0, rim[i, f], 0.0)
            rim[i, f] = left[:, :128]
            head = jnp.where(lane == 0, edge, left[:, :128])
            left = jnp.concatenate([head, left[:, 128:]], 1) if width > 128 else head
            done[i, f] = total - left

    @pl.when(t == tiles)
    def _():
        out[:, 0] = done[i]


def stencil(ids, flags, cot, vw, zc, mc, tail, smooth, halo, edges, old):
    _, levels, lon, lat = cot.shape
    width = WIDE
    tiles = lat // width
    nk = ids.shape[0]
    last = lambda t: jnp.minimum(t, tiles - 1)
    level = lambda t, i, ids: jnp.where(t == tiles, ids[nk - 1], ids[i])
    in_specs = [
        pl.BlockSpec((5, levels, lon, width), lambda t, i, ids, fl: (0, 0, 0, last(t))),
        pl.BlockSpec((levels, lon, width), lambda t, i, ids, fl: (0, 0, last(t))),
        pl.BlockSpec((1, lon, width), lambda t, i, ids, fl: (level(t, i, ids), 0, last(t))),
        pl.BlockSpec((1, lon, width), lambda t, i, ids, fl: (level(t, i, ids), 0, last(t))),
        pl.BlockSpec((lon, width), lambda t, i, ids, fl: (0, last(t))),
        pl.BlockSpec((5, 1, lon, 128), lambda t, i, ids, fl: (0, level(t, i, ids), 0, jnp.where(t < tiles - 1, 0, 1))),
        pl.BlockSpec((5, 1, 2, width), lambda t, i, ids, fl: (0, level(t, i, ids), 0, last(t))),
    ]
    in_specs += [pl.BlockSpec((5, lon, width), lambda t, i, ids, fl: (0, 0, last(t)))] * len(edges)
    args = [cot, vw, zc, mc, tail, smooth, halo, *edges]
    aliases = {}
    if old is not None:
        in_specs.append(pl.BlockSpec(memory_space=pl.ANY))
        args.append(old)
        aliases = {2 + len(args) - 1: 0}
    return pl.pallas_call(
        functools.partial(stencil_kernel, tiles, levels, len(edges), int(old is not None)),
        out_shape=jax.ShapeDtypeStruct(cot.shape, jnp.float32),
        grid_spec=pltpu.PrefetchScalarGridSpec(
            num_scalar_prefetch=2,
            grid=(tiles + 1, nk),
            in_specs=in_specs,
            out_specs=pl.BlockSpec(
                (5, 1, lon, width),
                lambda t, i, ids, fl: (0, jnp.where(t == 0, ids[0], ids[i]), 0, jnp.maximum(t - 1, 0)),
            ),
            scratch_shapes=[
                pltpu.VMEM((5, lon, width), jnp.float32),
                pltpu.VMEM((nk, 5, lon, width), jnp.float32),
                pltpu.VMEM((nk, 5, lon, 128), jnp.float32),
            ],
        ),
        input_output_aliases=aliases,
        compiler_params=pltpu.CompilerParams(vmem_limit_bytes=56 << 20),
        cost_estimate=pl.CostEstimate(
            flops=30 * nk * 5 * lon * lat, bytes_accessed=4 * nk * 13 * lon * lat, transcendentals=0
        ),
        name="stencil",
    )(ids, flags, *args)


def swap_levels(first, last):
    count = lax.axis_size("lev")
    if count == 2:
        seat = lax.axis_index("lev")
        got = lax.ppermute(jnp.where(seat == 0, last, first), "lev", [(0, 1), (1, 0)])
        return jnp.where(seat == 0, got, 0.0), jnp.where(seat == 1, got, 0.0)
    up = lax.ppermute(first, "lev", [(i + 1, i) for i in range(count - 1)])
    down = lax.ppermute(last, "lev", [(i, i + 1) for i in range(count - 1)])
    return up, down


def later_sum(local):
    count = lax.axis_size("lev")
    total = jnp.zeros_like(local)
    for r in range(1, count):
        total = total + lax.ppermute(local, "lev", [(i + r, i) for i in range(count - r)])
    return total


def adjoint_part(cot, vw):
    weighted = vw[None] * cot
    up, down = swap_levels(weighted[:, 0], weighted[:, -1])
    above = jnp.concatenate([weighted[:, 1:], up[:, None]], 1)
    under = jnp.concatenate([down[:, None], weighted[:, :-1]], 1)
    below = jnp.flip(jnp.cumsum(jnp.flip(cot[2], 0), 0), 0) + later_sum(cot[2].sum(0))[None]
    return (cot + (above - under)).at[3].add(-COUPLE_B * below)


def polar_cut(x):
    return jnp.concatenate([x[..., :POLAR], x[..., x.shape[-1] - POLAR :]], -1)


def body(cotangent, zonal_coef, merid_coef, vertical_wind, cutoff):
    levels, lon_dev, lat = cotangent.shape[1:]
    peers = lax.axis_size("lon")
    count = lax.axis_size("lev")
    seat = lax.axis_index("lev")

    polar_cot = jnp.swapaxes(polar_cut(cotangent), 2, 3)
    polar_vw = jnp.swapaxes(polar_cut(vertical_wind), 1, 2)
    polar = adjoint_part(polar_cot, polar_vw)
    rows = 2 * POLAR // peers
    grouped = polar.reshape(5 * levels, peers, rows, lon_dev)
    grouped = jnp.swapaxes(grouped, 0, 1).reshape(peers, 5 * levels * rows, lon_dev)

    ends = []
    for at in (lon_dev - 1, 0):
        ends.append(
            jnp.concatenate(
                [cotangent[:, :, at].reshape(5 * levels, lat), vertical_wind[:, at], zonal_coef[:, at]], 0
            )
        )
    up = [(i, (i + 1) % peers) for i in range(peers)]
    down = [(j, i) for i, j in up]
    beyond = jnp.stack([lax.ppermute(ends[0], "lon", up), lax.ppermute(ends[1], "lon", down)], 1)
    halo_cot = beyond[: 5 * levels].reshape(5, levels, 2, lat)
    halo_vw = beyond[5 * levels : 6 * levels]
    halo_zc = beyond[6 * levels :]
    halo_adj = adjoint_part(halo_cot, halo_vw)

    smoothed = polar_filter(grouped, cutoff, peers)
    smoothed = smoothed.reshape(peers, 5, levels, rows, lon_dev + 2)
    smoothed = smoothed.transpose(1, 2, 4, 0, 3).reshape(5, levels, lon_dev + 2, 2 * POLAR)
    inner = smoothed[:, :, 1 : lon_dev + 1]
    gap = jnp.zeros((5, levels, lon_dev, 256 - 2 * POLAR), jnp.float32)
    smooth = jnp.concatenate([inner[..., :POLAR], gap, inner[..., POLAR:]], 3)
    outer = smoothed[:, :, :: lon_dev + 1]
    halo_f = jnp.concatenate([outer[..., :POLAR], halo_adj[..., POLAR : lat - POLAR], outer[..., POLAR:]], 3)
    halo = jnp.stack(coupled(halo_zc, [halo_f[f] for f in range(5)], 0))

    tail = later_sum(cotangent[2].sum(0))
    first = vertical_wind[0][None] * cotangent[:, 0]
    last = vertical_wind[-1][None] * cotangent[:, -1]
    common = (cotangent, vertical_wind, zonal_coef, merid_coef, tail, smooth, halo)
    if count == 2 and levels > 1:
        got = lax.ppermute(jnp.where(seat == 0, last, first), "lev", [(0, 1), (1, 0)])
        ids = jnp.arange(levels - 1, dtype=jnp.int32) + seat
        flags = jnp.stack([(ids < levels - 1), (ids > 0)]).astype(jnp.float32)
        part = stencil(ids, flags, *common, (), None)
        ids = jnp.where(seat == 0, levels - 1, 0).astype(jnp.int32)[None]
        sign = jnp.where(seat == 0, 1.0, -1.0)[None]
        flags = jnp.stack([(ids < levels - 1), (ids > 0)]).astype(jnp.float32)
        flags = jnp.concatenate([flags, sign[None]], 0)
        return stencil(ids, flags, *common, (got,), part)
    above, under = swap_levels(first, last)
    ids = jnp.arange(levels, dtype=jnp.int32)
    flags = jnp.stack(
        [ids < levels - 1, ids > 0, ids == levels - 1, ids == 0]
    ).astype(jnp.float32) * jnp.array([1.0, 1.0, 1.0, -1.0], jnp.float32)[:, None]
    return stencil(ids, flags, *common, (above, under), None)


def solution(mesh):
    return jax.shard_map(
        body,
        mesh=mesh,
        in_specs=(
            P(None, "lev", "lon", None),
            P("lev", "lon", None),
            P("lev", "lon", None),
            P("lev", "lon", None),
            P(),
        ),
        out_specs=P(None, "lev", "lon", None),
        check_vma=False,
    )
```

```python
import functools
import math

import jax
import jax.numpy as jnp
from jax import lax
from jax.experimental import pallas as pl
from jax.experimental.pallas import tpu as pltpu
from jax.sharding import PartitionSpec as P

POLAR = 32
KMAX = 360
COUPLE_G = 0.3
COUPLE_H = 0.3
COUPLE_B = 0.2
MESH = pl.DeviceIdType.MESH
HIGHEST = lax.Precision.HIGHEST


def angles(left, right, period):
    turn = (left * right) % period
    phase = turn.astype(jnp.float32) * (2.0 * math.pi / period)
    return jnp.cos(phase), jnp.sin(phase)


def filter_kernel(
    peers, x_ref, fwd_ref, inv_ref, ct_ref, st_ref, mask_ref, out_ref, held, made,
    own_sem, send_a, recv_a, send_b, recv_b,
):
    me = lax.axis_index("lon")
    kpad = ct_ref.shape[2]
    barrier = pltpu.get_barrier_semaphore()

    def greet(o, _):
        pl.semaphore_signal(
            barrier, inc=1, device_id={"lon": lax.rem(me + o, peers)}, device_id_type=MESH
        )
        return 0

    lax.fori_loop(1, peers, greet, 0)
    pl.semaphore_wait(barrier, peers - 1)

    def out_copy(o):
        d = lax.rem(me + o, peers)
        return pltpu.make_async_remote_copy(
            src_ref=x_ref.at[d], dst_ref=held.at[me], send_sem=send_a.at[d],
            recv_sem=recv_a.at[me], device_id={"lon": d}, device_id_type=MESH,
        )

    def in_copy(o):
        s = lax.rem(me + o, peers)
        return pltpu.make_async_remote_copy(
            src_ref=x_ref.at[s], dst_ref=held.at[s], send_sem=send_a.at[s],
            recv_sem=recv_a.at[s], device_id={"lon": s}, device_id_type=MESH,
        )

    def back_copy(o):
        d = lax.rem(me + o, peers)
        return pltpu.make_async_remote_copy(
            src_ref=made.at[d], dst_ref=out_ref.at[me], send_sem=send_b.at[d],
            recv_sem=recv_b.at[me], device_id={"lon": d}, device_id_type=MESH,
        )

    def home_copy(o):
        s = lax.rem(me + o, peers)
        return pltpu.make_async_remote_copy(
            src_ref=made.at[s], dst_ref=out_ref.at[s], send_sem=send_b.at[s],
            recv_sem=recv_b.at[s], device_id={"lon": s}, device_id_type=MESH,
        )

    lax.fori_loop(1, peers, lambda o, c: (out_copy(o).start(), c)[1], 0)
    own = pltpu.make_async_copy(x_ref.at[me], held.at[me], own_sem)
    own.start()
    own.wait()
    lax.fori_loop(1, peers, lambda o, c: (in_copy(o).wait_recv(), c)[1], 0)

    cols = held.shape[1]
    zero = jnp.zeros((cols, kpad), jnp.float32)

    def gather(s, carry):
        a, b = carry
        both = jnp.dot(held[s], fwd_ref[...], precision=HIGHEST, preferred_element_type=jnp.float32)
        c, v = both[:, :kpad], both[:, kpad:]
        ct, st = ct_ref[s], st_ref[s]
        return a + (ct * c - st * v), b + (st * c + ct * v)

    a, b = lax.fori_loop(0, peers, gather, (zero, zero))
    a = a * mask_ref[...]
    b = b * mask_ref[...]

    def spread(d, carry):
        a, b = carry
        ct, st = ct_ref[d], st_ref[d]
        made[d] = jnp.dot(
            a * ct + b * st, inv_ref[0], precision=HIGHEST, preferred_element_type=jnp.float32
        ) + jnp.dot(
            b * ct - a * st, inv_ref[1], precision=HIGHEST, preferred_element_type=jnp.float32
        )
        return carry

    lax.fori_loop(0, peers, spread, (a, b))
    lax.fori_loop(1, peers, lambda o, c: (back_copy(o).start(), c)[1], 0)
    mine = pltpu.make_async_copy(made.at[me], out_ref.at[me], own_sem)
    mine.start()
    mine.wait()
    lax.fori_loop(1, peers, lambda o, c: (home_copy(o).wait_recv(), c)[1], 0)
    lax.fori_loop(1, peers, lambda o, c: (out_copy(o).wait_send(), c)[1], 0)
    lax.fori_loop(1, peers, lambda o, c: (back_copy(o).wait_send(), c)[1], 0)


def polar_filter(x, cutoff, peers):
    _, cols, lon_dev = x.shape
    nlon = peers * lon_dev
    rows = cutoff.shape[0] // peers
    kpad = (KMAX + 1 + 127) // 128 * 128
    wave = jnp.arange(kpad, dtype=jnp.int32)
    place = jnp.arange(lon_dev, dtype=jnp.int32)
    fwd = jnp.concatenate(angles(place[:, None], wave[None, :], nlon), axis=1)
    wide = jnp.arange(-1, lon_dev + 1, dtype=jnp.int32)
    inv = jnp.stack(angles(wave[:, None], wide[None, :] % nlon, nlon))
    seat = jnp.arange(peers, dtype=jnp.int32) * lon_dev
    ct, st = angles(seat[:, None, None], wave[None, None, :], nlon)
    mine = lax.dynamic_slice_in_dim(cutoff, lax.axis_index("lon") * rows, rows)
    weight = jnp.where(wave == 0, 1.0 / nlon, 2.0 / nlon)
    mask = jnp.where(wave[None, :] <= mine[:, None], weight[None, :], 0.0)
    mask = jnp.tile(mask, (cols // rows, 1))
    vmem = pl.BlockSpec(memory_space=pltpu.VMEM)
    dma = pltpu.SemaphoreType.DMA
    return pl.pallas_call(
        functools.partial(filter_kernel, peers),
        out_shape=jax.ShapeDtypeStruct((peers, cols, lon_dev + 2), jnp.float32),
        in_specs=[vmem] * 6,
        out_specs=vmem,
        scratch_shapes=[
            pltpu.VMEM((peers, cols, lon_dev), jnp.float32),
            pltpu.VMEM((peers, cols, lon_dev + 2), jnp.float32),
            dma(()), dma((peers,)), dma((peers,)), dma((peers,)), dma((peers,)),
        ],
        compiler_params=pltpu.CompilerParams(
            collective_id=0, has_side_effects=True, vmem_limit_bytes=24 << 20
        ),
        cost_estimate=pl.CostEstimate(flops=8_000_000_000, bytes_accessed=60_000_000, transcendentals=0),
        name="polar_filter",
    )(x, fwd, inv, ct, st, mask)


def to_rows(x):
    *lead, levels, lon, lat = x.shape
    n = len(lead)
    x = x.reshape(*lead, levels, lon, lat // 128, 128)
    x = x.transpose(*range(n), n + 1, n + 2, n, n + 3)
    return x.reshape(*lead, lon, lat // 128 * levels, 128)


def from_rows(x, levels):
    *lead, lon, rows, _ = x.shape
    n = len(lead)
    x = x.reshape(*lead, lon, rows // levels, levels, 128)
    x = x.transpose(*range(n), n + 2, n, n + 1, n + 3)
    return x.reshape(*lead, levels, lon, rows // levels * 128)


def chunk_of(lon):
    return max(d for d in range(1, 21) if lon % d == 0)


def edge_kernel(levels, choose, seat, cot, vw, *outs):
    fields, chunk, rows, _ = cot.shape
    tiles = rows // levels
    flat_c = cot.reshape(fields * chunk * rows, 128)
    flat_v = vw.reshape(chunk * rows, 128)
    *sends, tail = outs

    def level(ref, count, k):
        return ref[pl.ds(k, count * tiles, stride=levels), :] if levels > 1 else ref[...]

    def product(k, sign, out):
        c = level(flat_c, fields * chunk, k).reshape(fields, chunk, tiles, 128)
        v = level(flat_v, chunk, k).reshape(1, chunk, tiles, 128)
        out[...] = sign * (v * c)

    if choose:
        pl.when(seat[0] == 0)(lambda: product(levels - 1, -1.0, sends[0]))
        pl.when(seat[0] != 0)(lambda: product(0, 1.0, sends[0]))
    else:
        product(0, 1.0, sends[0])
        product(levels - 1, -1.0, sends[1])
    flat_t = cot.at[2].reshape(chunk * rows, 128)
    total = level(flat_t, chunk, 0)
    for k in range(1, levels):
        total = total + level(flat_t, chunk, k)
    tail[...] = total.reshape(chunk, tiles, 128)


def edges_of(seat, cot, vw, levels, choose):
    fields, lon, rows, _ = cot.shape
    tiles = rows // levels
    chunk = chunk_of(lon)
    n = 1 if choose else 2
    return pl.pallas_call(
        functools.partial(edge_kernel, levels, choose),
        out_shape=[jax.ShapeDtypeStruct((fields, lon, tiles, 128), jnp.float32)] * n
        + [jax.ShapeDtypeStruct((lon, tiles, 128), jnp.float32)],
        grid_spec=pltpu.PrefetchScalarGridSpec(
            num_scalar_prefetch=1,
            grid=(lon // chunk,),
            in_specs=[
                pl.BlockSpec((fields, chunk, rows, 128), lambda g, s: (0, g, 0, 0)),
                pl.BlockSpec((chunk, rows, 128), lambda g, s: (g, 0, 0)),
            ],
            out_specs=[pl.BlockSpec((fields, chunk, tiles, 128), lambda g, s: (0, g, 0, 0))] * n
            + [pl.BlockSpec((chunk, tiles, 128), lambda g, s: (g, 0, 0))],
        ),
        compiler_params=pltpu.CompilerParams(vmem_limit_bytes=24 << 20),
        cost_estimate=pl.CostEstimate(flops=10_000_000, bytes_accessed=22_000_000, transcendentals=0),
        name="edges",
    )(seat, cot, vw)


def coupled(coef, fields, first):
    flux = [coef * f for f in fields]
    flux[first] = flux[first] + COUPLE_H * fields[3]
    flux[3] = flux[3] + COUPLE_G * fields[first]
    return flux


def stencil_kernel(levels, steps, n_edge, seat, cot, vw, zc, mc, tail, smooth, halo, *rest):
    edges = rest[:n_edge]
    out, ready, final, wait, prior, spread, below_ref, sems, last_sem = rest[n_edge:]
    _, chunk, rows, _ = cot.shape
    tiles = rows // levels
    g = pl.program_id(0)
    slot = lax.rem(g, 2)
    lane = lax.broadcasted_iota(jnp.int32, (rows, 128), 1)
    row = lax.broadcasted_iota(jnp.int32, (rows, 128), 0)
    k = lax.rem(row, levels)
    cap_lane = lax.broadcasted_iota(jnp.int32, (2 * levels, 128), 1)
    cap_row = lax.broadcasted_iota(jnp.int32, (2 * levels, 128), 0)
    north = (cap_row < levels) & (cap_lane < POLAR)
    south = (cap_row >= levels) & (cap_lane >= 128 - POLAR)

    def first_copy():
        return pltpu.make_async_copy(
            ready.at[0, :, pl.ds(1, chunk - 1)], out.at[:, pl.ds(0, chunk - 1)], sems.at[0]
        )

    def copy(at):
        s = lax.rem(at, 2)
        return pltpu.make_async_copy(
            ready.at[s], out.at[:, pl.ds(at * chunk - 1, chunk)], sems.at[s]
        )

    @pl.when(g == 0)
    def _():
        spread[...] = jnp.zeros_like(spread)
        for f in range(5):
            prior[f] = halo[f, 0]
            wait[f] = jnp.zeros((rows, 128), jnp.float32)

    pl.when(g == 2)(lambda: first_copy().wait())
    pl.when(g > 2)(lambda: copy(g - 2).wait())

    def put(ref, at, value):
        if levels > 1:
            ref[pl.ds(at, tiles, stride=levels), :] = value
        else:
            ref[...] = value

    def one(l, _):
        for f in range(5):
            if n_edge == 1:
                pl.when(seat[0] == 0)(lambda: put(spread.at[0, f], levels - 1, edges[0][f, l]))
                pl.when(seat[0] != 0)(lambda: put(spread.at[0, f], 0, edges[0][f, l]))
            else:
                put(spread.at[0, f], levels - 1, edges[0][f, l])
                put(spread.at[1, f], 0, edges[1][f, l])
        for at in range(levels):
            put(below_ref, at, tail[l])
        wind = vw[l]
        base, fields = [], []
        for f in range(5):
            c = cot[f, l]
            w = wind * c
            a = c
            if levels > 1:
                up = jnp.where(k < levels - 1, pltpu.roll(w, rows - 1, 0), 0.0)
                a = a + (up - jnp.where(k > 0, pltpu.roll(w, 1, 0), 0.0))
            for n in range(n_edge):
                a = a + spread[n, f]
            if f == 3:
                theta = cot[2, l]
                below = below_ref[...] + theta
                for r in range(1, levels):
                    below = below + jnp.where(k < levels - r, pltpu.roll(theta, rows - r, 0), 0.0)
                a = a - COUPLE_B * below
            base.append(a)
            s = smooth[f, l]
            top = jnp.where(north, s, a[: 2 * levels])
            low = jnp.where(south, s, a[rows - 2 * levels :])
            fields.append(jnp.concatenate([top, a[2 * levels : rows - 2 * levels], low], 0))
        zonal = coupled(zc[l], fields, 0)
        merid = coupled(mc[l], fields, 1)
        for f in range(5):
            ready[slot, f, l] = wait[f] + zonal[f]
            left = pltpu.roll(merid[f], 1, 1)
            over = jnp.where(row < levels, 0.0, pltpu.roll(left, levels, 0))
            left = jnp.where(lane == 0, over, left)
            right = pltpu.roll(merid[f], 127, 1)
            over = jnp.where(row >= rows - levels, 0.0, pltpu.roll(right, rows - levels, 0))
            right = jnp.where(lane == 127, over, right)
            wait[f] = base[f] + (right - left) - prior[f]
            prior[f] = zonal[f]
        return 0

    lax.fori_loop(0, chunk, one, 0)
    pl.when(g == 0)(lambda: first_copy().start())
    pl.when(g > 0)(lambda: copy(g).start())

    @pl.when(g == steps - 1)
    def _():
        for f in range(5):
            final[f, 0] = wait[f] + halo[f, 1]
        end = pltpu.make_async_copy(final, out.at[:, pl.ds(steps * chunk - 1, 1)], last_sem)
        end.start()
        copy(g - 1).wait() if steps > 2 else first_copy().wait()
        copy(g).wait()
        end.wait()


def stencil(seat, cot, vw, zc, mc, tail, smooth, halo, edges, levels):
    _, lon, rows, _ = cot.shape
    tiles = rows // levels
    chunk = chunk_of(lon)
    steps = lon // chunk
    field = lambda n: pl.BlockSpec((5, chunk, n, 128), lambda g, s: (0, g, 0, 0))
    plain = lambda n: pl.BlockSpec((chunk, n, 128), lambda g, s: (g, 0, 0))
    return pl.pallas_call(
        functools.partial(stencil_kernel, levels, steps, len(edges)),
        out_shape=jax.ShapeDtypeStruct(cot.shape, jnp.float32),
        grid_spec=pltpu.PrefetchScalarGridSpec(
            num_scalar_prefetch=1,
            grid=(steps,),
            in_specs=[field(rows), plain(rows), plain(rows), plain(rows), plain(tiles), field(2 * levels),
                      pl.BlockSpec((5, 2, rows, 128), lambda g, s: (0, 0, 0, 0))]
            + [field(tiles)] * len(edges),
            out_specs=pl.BlockSpec(memory_space=pl.ANY),
            scratch_shapes=[
                pltpu.VMEM((2, 5, chunk, rows, 128), jnp.float32),
                pltpu.VMEM((5, 1, rows, 128), jnp.float32),
                pltpu.VMEM((5, rows, 128), jnp.float32),
                pltpu.VMEM((5, rows, 128), jnp.float32),
                pltpu.VMEM((len(edges), 5, rows, 128), jnp.float32),
                pltpu.VMEM((rows, 128), jnp.float32),
                pltpu.SemaphoreType.DMA((2,)),
                pltpu.SemaphoreType.DMA(()),
            ],
        ),
        compiler_params=pltpu.CompilerParams(vmem_limit_bytes=40 << 20),
        cost_estimate=pl.CostEstimate(
            flops=30 * 5 * lon * rows * 128, bytes_accessed=4 * 14 * lon * rows * 128, transcendentals=0
        ),
        name="stencil",
    )(seat, cot, vw, zc, mc, tail, smooth, halo, *edges)


def swap_levels(first, last):
    count = lax.axis_size("lev")
    if count == 2:
        seat = lax.axis_index("lev")
        got = lax.ppermute(jnp.where(seat == 0, last, first), "lev", [(0, 1), (1, 0)])
        return jnp.where(seat == 0, got, 0.0), jnp.where(seat == 1, got, 0.0)
    up = lax.ppermute(first, "lev", [(i + 1, i) for i in range(count - 1)])
    down = lax.ppermute(last, "lev", [(i, i + 1) for i in range(count - 1)])
    return up, down


def later_sum(local):
    count = lax.axis_size("lev")
    total = jnp.zeros_like(local)
    for r in range(1, count):
        total = total + lax.ppermute(local, "lev", [(i + r, i) for i in range(count - r)])
    return total


def adjoint_part(cot, vw):
    weighted = vw[None] * cot
    up, down = swap_levels(weighted[:, 0], weighted[:, -1])
    above = jnp.concatenate([weighted[:, 1:], up[:, None]], 1)
    under = jnp.concatenate([down[:, None], weighted[:, :-1]], 1)
    below = jnp.flip(jnp.cumsum(jnp.flip(cot[2], 0), 0), 0) + later_sum(cot[2].sum(0))[None]
    return (cot + (above - under)).at[3].add(-COUPLE_B * below)


def polar_cut(x):
    return jnp.concatenate([x[..., :POLAR], x[..., x.shape[-1] - POLAR :]], -1)


def body(cotangent, zonal_coef, merid_coef, vertical_wind, cutoff):
    levels, lon_dev, lat = cotangent.shape[1:]
    peers = lax.axis_size("lon")
    count = lax.axis_size("lev")
    seat = lax.axis_index("lev").astype(jnp.int32)[None]
    cot, vw = to_rows(cotangent), to_rows(vertical_wind)
    *sends, local = edges_of(seat, cot, vw, levels, count == 2)

    polar_cot = jnp.swapaxes(polar_cut(cotangent), 2, 3)
    polar_vw = jnp.swapaxes(polar_cut(vertical_wind), 1, 2)
    polar = adjoint_part(polar_cot, polar_vw)
    ends_adj = adjoint_part(cotangent[:, :, :: lon_dev - 1], vertical_wind[:, :: lon_dev - 1])

    polar, ends_adj, local, *sends = lax.optimization_barrier((polar, ends_adj, local, *sends))
    if count == 2:
        edges = [lax.ppermute(sends[0], "lev", [(0, 1), (1, 0)])]
    else:
        edges = [
            lax.ppermute(sends[0], "lev", [(i + 1, i) for i in range(count - 1)]),
            lax.ppermute(sends[1], "lev", [(i, i + 1) for i in range(count - 1)]),
        ]
    tail = later_sum(local)

    rows = 2 * POLAR // peers
    grouped = polar.reshape(5 * levels, peers, rows, lon_dev)
    grouped = jnp.swapaxes(grouped, 0, 1).reshape(peers, 5 * levels * rows, lon_dev)

    pack = jnp.concatenate([ends_adj.reshape(5 * levels, 2, lat), zonal_coef[:, :: lon_dev - 1]], 0)
    up = [(i, (i + 1) % peers) for i in range(peers)]
    down = [(j, i) for i, j in up]
    beyond = jnp.stack([lax.ppermute(pack[:, 1], "lon", up), lax.ppermute(pack[:, 0], "lon", down)], 1)
    halo_adj = beyond[: 5 * levels].reshape(5, levels, 2, lat)
    halo_zc = beyond[5 * levels :]

    smoothed = polar_filter(grouped, cutoff, peers)
    smoothed = smoothed.reshape(2, peers // 2, 5, levels, rows, lon_dev + 2)
    smoothed = smoothed.transpose(2, 5, 0, 3, 1, 4).reshape(5, lon_dev + 2, 2, levels, POLAR)
    north, south = smoothed[:, :, 0], smoothed[:, :, 1]
    gap = ((0, 0), (0, 0), (0, 0))
    smooth = jnp.concatenate(
        [jnp.pad(north, (*gap, (0, 128 - POLAR))), jnp.pad(south, (*gap, (128 - POLAR, 0)))], 2
    )[:, 1 : lon_dev + 1]
    outer = [jnp.swapaxes(x[:, :: lon_dev + 1], 1, 2) for x in (north, south)]
    halo_f = jnp.concatenate([outer[0], halo_adj[..., POLAR : lat - POLAR], outer[1]], 3)
    halo = jnp.stack(coupled(halo_zc, [halo_f[f] for f in range(5)], 0))
    out = stencil(
        seat, cot, vw, to_rows(zonal_coef), to_rows(merid_coef), tail, smooth, to_rows(halo), edges, levels
    )
    return from_rows(out, levels)


def solution(mesh):
    return jax.shard_map(
        body,
        mesh=mesh,
        in_specs=(
            P(None, "lev", "lon", None),
            P("lev", "lon", None),
            P("lev", "lon", None),
            P("lev", "lon", None),
            P(),
        ),
        out_specs=P(None, "lev", "lon", None),
        check_vma=False,
    )
```

```python
import functools
import math

import jax
import jax.numpy as jnp
import numpy as np
from jax import lax
from jax.experimental import pallas as pl
from jax.experimental.pallas import tpu as pltpu
from jax.sharding import PartitionSpec as P

POLAR = 32
KMAX = 360
COUPLE_G = 0.3
COUPLE_H = 0.3
COUPLE_B = 0.2
MESH = pl.DeviceIdType.MESH
HIGHEST = lax.Precision.HIGHEST


def angles(left, right, period):
    phase = (left * right) % period * (2.0 * math.pi / period)
    return np.cos(phase).astype(np.float32), np.sin(phase).astype(np.float32)


def filter_kernel(
    peers, x_ref, fwd_ref, inv_ref, ct_ref, st_ref, mask_ref, out_ref, held, made,
    own_sem, send_a, recv_a, send_b, recv_b,
):
    me = lax.axis_index("lon")
    kpad = ct_ref.shape[2]
    barrier = pltpu.get_barrier_semaphore()

    def greet(o, _):
        pl.semaphore_signal(
            barrier, inc=1, device_id={"lon": lax.rem(me + o, peers)}, device_id_type=MESH
        )
        return 0

    lax.fori_loop(1, peers, greet, 0)
    pl.semaphore_wait(barrier, peers - 1)

    def out_copy(o):
        d = lax.rem(me + o, peers)
        return pltpu.make_async_remote_copy(
            src_ref=x_ref.at[d], dst_ref=held.at[me], send_sem=send_a.at[d],
            recv_sem=recv_a.at[me], device_id={"lon": d}, device_id_type=MESH,
        )

    def in_copy(o):
        s = lax.rem(me + o, peers)
        return pltpu.make_async_remote_copy(
            src_ref=x_ref.at[s], dst_ref=held.at[s], send_sem=send_a.at[s],
            recv_sem=recv_a.at[s], device_id={"lon": s}, device_id_type=MESH,
        )

    def back_copy(o):
        d = lax.rem(me + o, peers)
        return pltpu.make_async_remote_copy(
            src_ref=made.at[d], dst_ref=out_ref.at[me], send_sem=send_b.at[d],
            recv_sem=recv_b.at[me], device_id={"lon": d}, device_id_type=MESH,
        )

    def home_copy(o):
        s = lax.rem(me + o, peers)
        return pltpu.make_async_remote_copy(
            src_ref=made.at[s], dst_ref=out_ref.at[s], send_sem=send_b.at[s],
            recv_sem=recv_b.at[s], device_id={"lon": s}, device_id_type=MESH,
        )

    lax.fori_loop(1, peers, lambda o, c: (out_copy(o).start(), c)[1], 0)
    own = pltpu.make_async_copy(x_ref.at[me], held.at[me], own_sem)
    own.start()
    own.wait()
    lax.fori_loop(1, peers, lambda o, c: (in_copy(o).wait_recv(), c)[1], 0)

    cols = held.shape[1]
    zero = jnp.zeros((cols, kpad), jnp.float32)

    def gather(s, carry):
        a, b = carry
        both = jnp.dot(held[s], fwd_ref[...], precision=HIGHEST, preferred_element_type=jnp.float32)
        c, v = both[:, :kpad], both[:, kpad:]
        ct, st = ct_ref[s], st_ref[s]
        return a + (ct * c - st * v), b + (st * c + ct * v)

    a, b = lax.fori_loop(0, peers, gather, (zero, zero))
    a = a * mask_ref[...]
    b = b * mask_ref[...]

    def spread(d, carry):
        a, b = carry
        ct, st = ct_ref[d], st_ref[d]
        made[d] = jnp.dot(
            a * ct + b * st, inv_ref[0], precision=HIGHEST, preferred_element_type=jnp.float32
        ) + jnp.dot(
            b * ct - a * st, inv_ref[1], precision=HIGHEST, preferred_element_type=jnp.float32
        )
        return carry

    lax.fori_loop(0, peers, spread, (a, b))
    lax.fori_loop(1, peers, lambda o, c: (back_copy(o).start(), c)[1], 0)
    mine = pltpu.make_async_copy(made.at[me], out_ref.at[me], own_sem)
    mine.start()
    mine.wait()
    lax.fori_loop(1, peers, lambda o, c: (home_copy(o).wait_recv(), c)[1], 0)
    lax.fori_loop(1, peers, lambda o, c: (out_copy(o).wait_send(), c)[1], 0)
    lax.fori_loop(1, peers, lambda o, c: (back_copy(o).wait_send(), c)[1], 0)


def polar_filter(x, cutoff, peers):
    _, cols, lon_dev = x.shape
    nlon = peers * lon_dev
    rows = cutoff.shape[0] // peers
    kpad = (KMAX + 1 + 127) // 128 * 128
    wave = np.arange(kpad)
    fwd = np.concatenate(angles(np.arange(lon_dev)[:, None], wave[None, :], nlon), axis=1)
    inv = np.stack(angles(wave[:, None], np.arange(-1, lon_dev + 1)[None, :] % nlon, nlon))
    ct, st = angles(np.arange(peers)[:, None, None] * lon_dev, wave[None, None, :], nlon)
    mine = lax.dynamic_slice_in_dim(cutoff, lax.axis_index("lon") * rows, rows)
    weight = np.where(wave == 0, 1.0 / nlon, 2.0 / nlon).astype(np.float32)
    mask = jnp.where(jnp.asarray(wave, jnp.int32)[None, :] <= mine[:, None], weight[None, :], 0.0)
    mask = jnp.tile(mask, (cols // rows, 1))
    vmem = pl.BlockSpec(memory_space=pltpu.VMEM)
    dma = pltpu.SemaphoreType.DMA
    return pl.pallas_call(
        functools.partial(filter_kernel, peers),
        out_shape=jax.ShapeDtypeStruct((peers, cols, lon_dev + 2), jnp.float32),
        in_specs=[vmem] * 6,
        out_specs=vmem,
        scratch_shapes=[
            pltpu.VMEM((peers, cols, lon_dev), jnp.float32),
            pltpu.VMEM((peers, cols, lon_dev + 2), jnp.float32),
            dma(()), dma((peers,)), dma((peers,)), dma((peers,)), dma((peers,)),
        ],
        compiler_params=pltpu.CompilerParams(
            collective_id=0, has_side_effects=True, vmem_limit_bytes=24 << 20
        ),
        cost_estimate=pl.CostEstimate(flops=8_000_000_000, bytes_accessed=60_000_000, transcendentals=0),
        name="polar_filter",
    )(x, fwd, inv, ct, st, mask)


def to_rows(x):
    *lead, levels, lon, lat = x.shape
    n = len(lead)
    x = x.reshape(*lead, levels, lon, lat // 128, 128)
    x = x.transpose(*range(n), n + 1, n + 2, n, n + 3)
    return x.reshape(*lead, lon, lat // 128 * levels, 128)


def from_rows(x, levels):
    *lead, lon, rows, _ = x.shape
    n = len(lead)
    x = x.reshape(*lead, lon, rows // levels, levels, 128)
    x = x.transpose(*range(n), n + 2, n, n + 1, n + 3)
    return x.reshape(*lead, levels, lon, rows // levels * 128)


def chunk_of(lon):
    return max(d for d in range(1, 21) if lon % d == 0)


def edge_kernel(levels, choose, seat, cot, vw, *outs):
    fields, chunk, rows, _ = cot.shape
    tiles = rows // levels
    flat_c = cot.reshape(fields * chunk * rows, 128)
    flat_v = vw.reshape(chunk * rows, 128)
    sends = outs[: 1 if choose else 2]

    def level(ref, count, k):
        return ref[pl.ds(k, count * tiles, stride=levels), :] if levels > 1 else ref[...]

    def product(k, sign, out):
        c = level(flat_c, fields * chunk, k).reshape(fields, chunk, tiles, 128)
        v = level(flat_v, chunk, k).reshape(1, chunk, tiles, 128)
        out[:fields] = sign * (v * c)

    flat_t = cot.at[2].reshape(chunk * rows, 128)
    total = level(flat_t, chunk, 0)
    for k in range(1, levels):
        total = total + level(flat_t, chunk, k)
    total = total.reshape(chunk, tiles, 128)
    if choose:
        sends[0][fields] = jnp.where(seat[0] == 0, 0.0, total)
        pl.when(seat[0] == 0)(lambda: product(levels - 1, -1.0, sends[0]))
        pl.when(seat[0] != 0)(lambda: product(0, 1.0, sends[0]))
    else:
        product(0, 1.0, sends[0])
        product(levels - 1, -1.0, sends[1])
        outs[2][...] = total


def edges_of(seat, cot, vw, levels, choose):
    fields, lon, rows, _ = cot.shape
    tiles = rows // levels
    chunk = chunk_of(lon)
    n = 1 if choose else 2
    wide = fields + 1 if choose else fields
    return pl.pallas_call(
        functools.partial(edge_kernel, levels, choose),
        out_shape=[jax.ShapeDtypeStruct((wide, lon, tiles, 128), jnp.float32)] * n
        + [jax.ShapeDtypeStruct((lon, tiles, 128), jnp.float32)] * (n - 1),
        grid_spec=pltpu.PrefetchScalarGridSpec(
            num_scalar_prefetch=1,
            grid=(lon // chunk,),
            in_specs=[
                pl.BlockSpec((fields, chunk, rows, 128), lambda g, s: (0, g, 0, 0)),
                pl.BlockSpec((chunk, rows, 128), lambda g, s: (g, 0, 0)),
            ],
            out_specs=[pl.BlockSpec((wide, chunk, tiles, 128), lambda g, s: (0, g, 0, 0))] * n
            + [pl.BlockSpec((chunk, tiles, 128), lambda g, s: (g, 0, 0))] * (n - 1),
        ),
        compiler_params=pltpu.CompilerParams(vmem_limit_bytes=24 << 20),
        cost_estimate=pl.CostEstimate(flops=10_000_000, bytes_accessed=22_000_000, transcendentals=0),
        name="edges",
    )(seat, cot, vw)


def coupled(coef, fields, first):
    flux = [coef * f for f in fields]
    flux[first] = flux[first] + COUPLE_H * fields[3]
    flux[3] = flux[3] + COUPLE_G * fields[first]
    return flux


def stencil_kernel(levels, steps, n_edge, seat, cot, vw, zc, mc, smooth, halo, *rest):
    edges = rest[:n_edge]
    tail = edges[0].at[5] if n_edge == 1 else rest[n_edge]
    rest = rest[1:] if n_edge > 1 else rest
    edge_at = (1 - seat[0]) * (levels - 1)
    out, ready, final, wait, prior, spread, below_ref, sems, last_sem = rest[n_edge:]
    _, chunk, rows, _ = cot.shape
    tiles = rows // levels
    g = pl.program_id(0)
    slot = lax.rem(g, 2)
    lane = lax.broadcasted_iota(jnp.int32, (rows, 128), 1)
    row = lax.broadcasted_iota(jnp.int32, (rows, 128), 0)
    k = lax.rem(row, levels)
    cap_lane = lax.broadcasted_iota(jnp.int32, (2 * levels, 128), 1)
    cap_row = lax.broadcasted_iota(jnp.int32, (2 * levels, 128), 0)
    north = (cap_row < levels) & (cap_lane < POLAR)
    south = (cap_row >= levels) & (cap_lane >= 128 - POLAR)

    def first_copy():
        return pltpu.make_async_copy(
            ready.at[0, :, pl.ds(1, chunk - 1)], out.at[:, pl.ds(0, chunk - 1)], sems.at[0]
        )

    def copy(at):
        s = lax.rem(at, 2)
        return pltpu.make_async_copy(
            ready.at[s], out.at[:, pl.ds(at * chunk - 1, chunk)], sems.at[s]
        )

    @pl.when(g == 0)
    def _():
        spread[...] = jnp.zeros_like(spread)
        for f in range(5):
            prior[f] = halo[f, 0]
            wait[f] = jnp.zeros((rows, 128), jnp.float32)

    pl.when(g == 2)(lambda: first_copy().wait())
    pl.when(g > 2)(lambda: copy(g - 2).wait())

    def put(ref, at, value):
        if levels > 1:
            ref[pl.ds(at, tiles, stride=levels), :] = value
        else:
            ref[...] = value

    def one(l, _):
        for f in range(5):
            if n_edge == 1:
                put(spread.at[0, f], edge_at, edges[0][f, l])
            else:
                put(spread.at[0, f], levels - 1, edges[0][f, l])
                put(spread.at[1, f], 0, edges[1][f, l])
        for at in range(levels):
            put(below_ref, at, tail[l])
        wind = vw[l]
        base, fields = [], []
        for f in range(5):
            c = cot[f, l]
            w = wind * c
            a = c
            if levels > 1:
                up = jnp.where(k < levels - 1, pltpu.roll(w, rows - 1, 0), 0.0)
                a = a + (up - jnp.where(k > 0, pltpu.roll(w, 1, 0), 0.0))
            for n in range(n_edge):
                a = a + spread[n, f]
            if f == 3:
                theta = cot[2, l]
                below = below_ref[...] + theta
                for r in range(1, levels):
                    below = below + jnp.where(k < levels - r, pltpu.roll(theta, rows - r, 0), 0.0)
                a = a - COUPLE_B * below
            base.append(a)
            s = smooth[f, l]
            top = jnp.where(north, s, a[: 2 * levels])
            low = jnp.where(south, s, a[rows - 2 * levels :])
            fields.append(jnp.concatenate([top, a[2 * levels : rows - 2 * levels], low], 0))
        zonal = coupled(zc[l], fields, 0)
        merid = coupled(mc[l], fields, 1)
        for f in range(5):
            ready[slot, f, l] = wait[f] + zonal[f]
            left = pltpu.roll(merid[f], 1, 1)
            over = jnp.where(row < levels, 0.0, pltpu.roll(left, levels, 0))
            left = jnp.where(lane == 0, over, left)
            right = pltpu.roll(merid[f], 127, 1)
            over = jnp.where(row >= rows - levels, 0.0, pltpu.roll(right, rows - levels, 0))
            right = jnp.where(lane == 127, over, right)
            wait[f] = base[f] + (right - left) - prior[f]
            prior[f] = zonal[f]
        return 0

    lax.fori_loop(0, chunk, one, 0)
    pl.when(g == 0)(lambda: first_copy().start())
    pl.when(g > 0)(lambda: copy(g).start())

    @pl.when(g == steps - 1)
    def _():
        for f in range(5):
            final[f, 0] = wait[f] + halo[f, 1]
        end = pltpu.make_async_copy(final, out.at[:, pl.ds(steps * chunk - 1, 1)], last_sem)
        end.start()
        copy(g - 1).wait() if steps > 2 else first_copy().wait()
        copy(g).wait()
        end.wait()


def stencil(seat, cot, vw, zc, mc, smooth, halo, edges, levels):
    _, lon, rows, _ = cot.shape
    tiles = rows // levels
    chunk = chunk_of(lon)
    steps = lon // chunk
    field = lambda n: pl.BlockSpec((5, chunk, n, 128), lambda g, s: (0, g, 0, 0))
    plain = lambda n: pl.BlockSpec((chunk, n, 128), lambda g, s: (g, 0, 0))
    return pl.pallas_call(
        functools.partial(stencil_kernel, levels, steps, min(len(edges), 2)),
        out_shape=jax.ShapeDtypeStruct(cot.shape, jnp.float32),
        grid_spec=pltpu.PrefetchScalarGridSpec(
            num_scalar_prefetch=1,
            grid=(steps,),
            in_specs=[field(rows), plain(rows), plain(rows), plain(rows), field(2 * levels),
                      pl.BlockSpec((5, 2, rows, 128), lambda g, s: (0, 0, 0, 0))]
            + [pl.BlockSpec((6, chunk, tiles, 128), lambda g, s: (0, g, 0, 0))]
            if len(edges) == 1
            else [field(rows), plain(rows), plain(rows), plain(rows), field(2 * levels),
                  pl.BlockSpec((5, 2, rows, 128), lambda g, s: (0, 0, 0, 0)),
                  field(tiles), field(tiles), plain(tiles)],
            out_specs=pl.BlockSpec(memory_space=pl.ANY),
            scratch_shapes=[
                pltpu.VMEM((2, 5, chunk, rows, 128), jnp.float32),
                pltpu.VMEM((5, 1, rows, 128), jnp.float32),
                pltpu.VMEM((5, rows, 128), jnp.float32),
                pltpu.VMEM((5, rows, 128), jnp.float32),
                pltpu.VMEM((min(len(edges), 2), 5, rows, 128), jnp.float32),
                pltpu.VMEM((rows, 128), jnp.float32),
                pltpu.SemaphoreType.DMA((2,)),
                pltpu.SemaphoreType.DMA(()),
            ],
        ),
        compiler_params=pltpu.CompilerParams(vmem_limit_bytes=40 << 20),
        cost_estimate=pl.CostEstimate(
            flops=30 * 5 * lon * rows * 128, bytes_accessed=4 * 14 * lon * rows * 128, transcendentals=0
        ),
        name="stencil",
    )(seat, cot, vw, zc, mc, smooth, halo, *edges)


def swap_levels(first, last, total):
    count = lax.axis_size("lev")
    if count == 2:
        seat = lax.axis_index("lev")
        lead = jnp.concatenate([first, total[None]], 0)
        trail = jnp.concatenate([last, jnp.zeros_like(total)[None]], 0)
        got = lax.ppermute(jnp.where(seat == 0, trail, lead), "lev", [(0, 1), (1, 0)])
        return jnp.where(seat == 0, got[:5], 0.0), jnp.where(seat == 1, got[:5], 0.0), got[5]
    up = lax.ppermute(first, "lev", [(i + 1, i) for i in range(count - 1)])
    down = lax.ppermute(last, "lev", [(i, i + 1) for i in range(count - 1)])
    return up, down, later_sum(total)


def later_sum(local):
    count = lax.axis_size("lev")
    total = jnp.zeros_like(local)
    for r in range(1, count):
        total = total + lax.ppermute(local, "lev", [(i + r, i) for i in range(count - r)])
    return total


def ask_levels(cot, vw):
    return swap_levels(vw[0] * cot[:, 0], vw[-1] * cot[:, -1], cot[2].sum(0))


def adjoint_part(cot, vw, up, down, later):
    weighted = vw[None] * cot
    above = jnp.concatenate([weighted[:, 1:], up[:, None]], 1)
    under = jnp.concatenate([down[:, None], weighted[:, :-1]], 1)
    below = [later + cot[2, -1]]
    for k in range(cot.shape[1] - 2, -1, -1):
        below.insert(0, below[0] + cot[2, k])
    parts = cot + (above - under)
    return jnp.concatenate(
        [parts[:3], parts[3:4] - COUPLE_B * jnp.stack(below)[None], parts[4:]], 0
    )


def polar_cut(x):
    return jnp.concatenate([x[..., :POLAR], x[..., x.shape[-1] - POLAR :]], -1)


def body(cotangent, zonal_coef, merid_coef, vertical_wind, cutoff):
    levels, lon_dev, lat = cotangent.shape[1:]
    peers = lax.axis_size("lon")
    count = lax.axis_size("lev")
    seat = lax.axis_index("lev").astype(jnp.int32)[None]
    cot, vw = to_rows(cotangent), to_rows(vertical_wind)
    polar_cot = jnp.swapaxes(polar_cut(cotangent), 2, 3)
    polar_vw = jnp.swapaxes(polar_cut(vertical_wind), 1, 2)
    polar_got = ask_levels(polar_cot, polar_vw)
    ends_cot, ends_vw = cotangent[:, :, :: lon_dev - 1], vertical_wind[:, :: lon_dev - 1]
    ends_got = ask_levels(ends_cot, ends_vw)

    sends = edges_of(seat, cot, vw, levels, count == 2)
    polar_got, ends_got, sends = lax.optimization_barrier((polar_got, ends_got, sends))
    if count == 2:
        edges = [lax.ppermute(sends[0], "lev", [(0, 1), (1, 0)])]
    else:
        edges = [
            lax.ppermute(sends[0], "lev", [(i + 1, i) for i in range(count - 1)]),
            lax.ppermute(sends[1], "lev", [(i, i + 1) for i in range(count - 1)]),
            later_sum(sends[2]),
        ]
    polar = adjoint_part(polar_cot, polar_vw, *polar_got)
    ends_adj = adjoint_part(ends_cot, ends_vw, *ends_got)

    rows = 2 * POLAR // peers
    grouped = polar.reshape(5 * levels, peers, rows, lon_dev)
    grouped = jnp.swapaxes(grouped, 0, 1).reshape(peers, 5 * levels * rows, lon_dev)

    pack = jnp.concatenate([ends_adj.reshape(5 * levels, 2, lat), zonal_coef[:, :: lon_dev - 1]], 0)
    up = [(i, (i + 1) % peers) for i in range(peers)]
    down = [(j, i) for i, j in up]
    beyond = jnp.stack([lax.ppermute(pack[:, 1], "lon", up), lax.ppermute(pack[:, 0], "lon", down)], 1)
    halo_adj = beyond[: 5 * levels].reshape(5, levels, 2, lat)
    halo_zc = beyond[5 * levels :]

    smoothed = polar_filter(grouped, cutoff, peers)
    smoothed = smoothed.reshape(2, peers // 2, 5, levels, rows, lon_dev + 2)
    smoothed = smoothed.transpose(2, 5, 0, 3, 1, 4).reshape(5, lon_dev + 2, 2, levels, POLAR)
    north, south = smoothed[:, :, 0], smoothed[:, :, 1]
    gap = ((0, 0), (0, 0), (0, 0))
    smooth = jnp.concatenate(
        [jnp.pad(north, (*gap, (0, 128 - POLAR))), jnp.pad(south, (*gap, (128 - POLAR, 0)))], 2
    )[:, 1 : lon_dev + 1]
    outer = [jnp.swapaxes(x[:, :: lon_dev + 1], 1, 2) for x in (north, south)]
    halo_f = jnp.concatenate([outer[0], halo_adj[..., POLAR : lat - POLAR], outer[1]], 3)
    halo = jnp.stack(coupled(halo_zc, [halo_f[f] for f in range(5)], 0))
    out = stencil(
        seat, cot, vw, to_rows(zonal_coef), to_rows(merid_coef), smooth, to_rows(halo), edges, levels
    )
    return from_rows(out, levels)


def solution(mesh):
    return jax.shard_map(
        body,
        mesh=mesh,
        in_specs=(
            P(None, "lev", "lon", None),
            P("lev", "lon", None),
            P("lev", "lon", None),
            P("lev", "lon", None),
            P(),
        ),
        out_specs=P(None, "lev", "lon", None),
        check_vma=False,
    )
```

```python
import functools
import math

import jax
import jax.numpy as jnp
import numpy as np
from jax import lax
from jax.experimental import pallas as pl
from jax.experimental.pallas import tpu as pltpu
from jax.sharding import PartitionSpec as P

POLAR = 32
KMAX = 360
COUPLE_G = 0.3
COUPLE_H = 0.3
COUPLE_B = 0.2
MESH = pl.DeviceIdType.MESH
HIGHEST = lax.Precision.HIGHEST


def angles(left, right, period):
    phase = (left * right) % period * (2.0 * math.pi / period)
    return np.cos(phase).astype(np.float32), np.sin(phase).astype(np.float32)


def filter_kernel(
    peers, packed, x_ref, fwd_ref, inv_ref, ct_ref, st_ref, mask_ref, out_ref, held, made,
    own_sem, send_a, recv_a, send_b, recv_b,
):
    me = lax.axis_index("lon")
    kpad = ct_ref.shape[2]
    barrier = pltpu.get_barrier_semaphore()

    def greet(o, _):
        pl.semaphore_signal(
            barrier, inc=1, device_id={"lon": lax.rem(me + o, peers)}, device_id_type=MESH
        )
        return 0

    lax.fori_loop(1, peers, greet, 0)
    pl.semaphore_wait(barrier, peers - 1)

    def out_copy(o):
        d = lax.rem(me + o, peers)
        return pltpu.make_async_remote_copy(
            src_ref=x_ref.at[d], dst_ref=held.at[me], send_sem=send_a.at[d],
            recv_sem=recv_a.at[me], device_id={"lon": d}, device_id_type=MESH,
        )

    def in_copy(o):
        s = lax.rem(me + o, peers)
        return pltpu.make_async_remote_copy(
            src_ref=x_ref.at[s], dst_ref=held.at[s], send_sem=send_a.at[s],
            recv_sem=recv_a.at[s], device_id={"lon": s}, device_id_type=MESH,
        )

    def back_copy(o):
        d = lax.rem(me + o, peers)
        return pltpu.make_async_remote_copy(
            src_ref=made.at[d], dst_ref=out_ref.at[me], send_sem=send_b.at[d],
            recv_sem=recv_b.at[me], device_id={"lon": d}, device_id_type=MESH,
        )

    def home_copy(o):
        s = lax.rem(me + o, peers)
        return pltpu.make_async_remote_copy(
            src_ref=made.at[s], dst_ref=out_ref.at[s], send_sem=send_b.at[s],
            recv_sem=recv_b.at[s], device_id={"lon": s}, device_id_type=MESH,
        )

    lax.fori_loop(1, peers, lambda o, c: (out_copy(o).start(), c)[1], 0)
    own = pltpu.make_async_copy(x_ref.at[me], held.at[me], own_sem)
    own.start()
    own.wait()
    cols = mask_ref.shape[0]
    half = cols // 2
    zero = jnp.zeros((cols, kpad), jnp.float32)
    dot = functools.partial(jnp.dot, precision=HIGHEST, preferred_element_type=jnp.float32)

    def gather(s, carry):
        a, b = carry
        if packed:
            ends = held[s, cols:]
            ends = jnp.concatenate([ends[:, :64], ends[:, 64:]], 0)
            both = dot(held[s, :cols], fwd_ref[:128]) + dot(ends, fwd_ref[128:])
        else:
            both = dot(held[s], fwd_ref[...])
        c, v = both[:, :kpad], both[:, kpad:]
        ct, st = ct_ref[s], st_ref[s]
        return a + (ct * c - st * v), b + (st * c + ct * v)

    def arrive(o, carry):
        in_copy(o).wait_recv()
        return gather(lax.rem(me + o, peers), carry)

    a, b = lax.fori_loop(1, peers, arrive, gather(me, (zero, zero)))
    a = a * mask_ref[...]
    b = b * mask_ref[...]

    def spread(d):
        ct, st = ct_ref[d], st_ref[d]
        p, q = a * ct + b * st, b * ct - a * st
        if packed:
            y = dot(p, inv_ref[0]) + dot(q, inv_ref[1])
            made[d, :cols] = y[:, :128]
            made[d, cols:] = jnp.concatenate([y[:half, 128:], y[half:, 128:]], 1)
        else:
            made[d] = dot(p, inv_ref[0]) + dot(q, inv_ref[1])

    def depart(o, _):
        spread(lax.rem(me + o, peers))
        pl.when(o > 1)(lambda: back_copy(o - 1).start())
        return 0

    lax.fori_loop(1, peers, depart, 0)
    spread(me)
    back_copy(peers - 1).start()
    mine = pltpu.make_async_copy(made.at[me], out_ref.at[me], own_sem)
    mine.start()
    mine.wait()
    lax.fori_loop(1, peers, lambda o, c: (home_copy(o).wait_recv(), c)[1], 0)
    lax.fori_loop(1, peers, lambda o, c: (out_copy(o).wait_send(), c)[1], 0)
    lax.fori_loop(1, peers, lambda o, c: (back_copy(o).wait_send(), c)[1], 0)


def polar_filter(x, cutoff, peers):
    _, cols, lon_dev = x.shape
    nlon = peers * lon_dev
    rows = cutoff.shape[0] // peers
    kpad = (KMAX + 1 + 127) // 128 * 128
    wave = np.arange(kpad)
    fwd = np.concatenate(angles(np.arange(lon_dev)[:, None], wave[None, :], nlon), axis=1)
    inv = np.stack(angles(wave[:, None], np.arange(-1, lon_dev + 1)[None, :] % nlon, nlon))
    over, wider = lon_dev - 128, lon_dev + 2 - 128
    packed = over > 0 and wider <= 64 and cols % 16 == 0
    half = cols // 2
    if packed:
        fwd = np.pad(fwd, ((0, 64 - over), (0, 0)))
        inv = np.pad(inv, ((0, 0), (0, 0), (0, 64 - wider)))
        ends = jnp.pad(x[..., 128:], ((0, 0), (0, 0), (0, 64 - over)))
        x = jnp.concatenate([x[..., :128], jnp.concatenate([ends[:, :half], ends[:, half:]], 2)], 1)
        shape = (peers, cols + half, 128)
    else:
        shape = (peers, cols, lon_dev + 2)
    ct, st = angles(np.arange(peers)[:, None, None] * lon_dev, wave[None, None, :], nlon)
    mine = lax.dynamic_slice_in_dim(cutoff, lax.axis_index("lon") * rows, rows)
    weight = np.where(wave == 0, 1.0 / nlon, 2.0 / nlon).astype(np.float32)
    mask = jnp.where(jnp.asarray(wave, jnp.int32)[None, :] <= mine[:, None], weight[None, :], 0.0)
    mask = jnp.tile(mask, (cols // rows, 1))
    vmem = pl.BlockSpec(memory_space=pltpu.VMEM)
    dma = pltpu.SemaphoreType.DMA
    y = pl.pallas_call(
        functools.partial(filter_kernel, peers, packed),
        out_shape=jax.ShapeDtypeStruct(shape, jnp.float32),
        in_specs=[vmem] * 6,
        out_specs=vmem,
        scratch_shapes=[
            pltpu.VMEM(x.shape, jnp.float32),
            pltpu.VMEM(shape, jnp.float32),
            dma(()), dma((peers,)), dma((peers,)), dma((peers,)), dma((peers,)),
        ],
        compiler_params=pltpu.CompilerParams(
            collective_id=0, has_side_effects=True, vmem_limit_bytes=24 << 20
        ),
        cost_estimate=pl.CostEstimate(flops=8_000_000_000, bytes_accessed=60_000_000, transcendentals=0),
        name="polar_filter",
    )(x, fwd, inv, ct, st, mask)
    if not packed:
        return y
    ends = jnp.concatenate([y[:, cols:, :wider], y[:, cols:, 64 : 64 + wider]], 1)
    return jnp.concatenate([y[:, :cols], ends], 2)


def to_rows(x):
    *lead, levels, lon, lat = x.shape
    n = len(lead)
    x = x.reshape(*lead, levels, lon, lat // 128, 128)
    x = x.transpose(*range(n), n + 1, n + 2, n, n + 3)
    return x.reshape(*lead, lon, lat // 128 * levels, 128)


def from_rows(x, levels):
    *lead, lon, rows, _ = x.shape
    n = len(lead)
    x = x.reshape(*lead, lon, rows // levels, levels, 128)
    x = x.transpose(*range(n), n + 2, n, n + 1, n + 3)
    return x.reshape(*lead, levels, lon, rows // levels * 128)


def chunk_of(lon):
    return max(d for d in range(1, 21) if lon % d == 0)


def edge_kernel(levels, choose, seat, cot, vw, *outs):
    fields, chunk, rows, _ = cot.shape
    tiles = rows // levels
    flat_c = cot.reshape(fields * chunk * rows, 128)
    flat_v = vw.reshape(chunk * rows, 128)
    sends = outs[: 1 if choose else 2]

    def level(ref, count, k):
        return ref[pl.ds(k, count * tiles, stride=levels), :] if levels > 1 else ref[...]

    def product(k, sign, out):
        c = level(flat_c, fields * chunk, k).reshape(fields, chunk, tiles, 128)
        v = level(flat_v, chunk, k).reshape(1, chunk, tiles, 128)
        out[:fields] = sign * (v * c)

    flat_t = cot.at[2].reshape(chunk * rows, 128)
    total = level(flat_t, chunk, 0)
    for k in range(1, levels):
        total = total + level(flat_t, chunk, k)
    total = total.reshape(chunk, tiles, 128)
    if choose:
        sends[0][fields] = jnp.where(seat[0] == 0, 0.0, total)
        pl.when(seat[0] == 0)(lambda: product(levels - 1, -1.0, sends[0]))
        pl.when(seat[0] != 0)(lambda: product(0, 1.0, sends[0]))
    else:
        product(0, 1.0, sends[0])
        product(levels - 1, -1.0, sends[1])
        outs[2][...] = total


def edges_of(seat, cot, vw, levels, choose):
    fields, lon, rows, _ = cot.shape
    tiles = rows // levels
    chunk = chunk_of(lon)
    n = 1 if choose else 2
    wide = fields + 1 if choose else fields
    return pl.pallas_call(
        functools.partial(edge_kernel, levels, choose),
        out_shape=[jax.ShapeDtypeStruct((wide, lon, tiles, 128), jnp.float32)] * n
        + [jax.ShapeDtypeStruct((lon, tiles, 128), jnp.float32)] * (n - 1),
        grid_spec=pltpu.PrefetchScalarGridSpec(
            num_scalar_prefetch=1,
            grid=(lon // chunk,),
            in_specs=[
                pl.BlockSpec((fields, chunk, rows, 128), lambda g, s: (0, g, 0, 0)),
                pl.BlockSpec((chunk, rows, 128), lambda g, s: (g, 0, 0)),
            ],
            out_specs=[pl.BlockSpec((wide, chunk, tiles, 128), lambda g, s: (0, g, 0, 0))] * n
            + [pl.BlockSpec((chunk, tiles, 128), lambda g, s: (g, 0, 0))] * (n - 1),
        ),
        compiler_params=pltpu.CompilerParams(vmem_limit_bytes=24 << 20),
        cost_estimate=pl.CostEstimate(flops=10_000_000, bytes_accessed=22_000_000, transcendentals=0),
        name="edges",
    )(seat, cot, vw)


def coupled(coef, fields, first):
    flux = [coef * f for f in fields]
    flux[first] = flux[first] + COUPLE_H * fields[3]
    flux[3] = flux[3] + COUPLE_G * fields[first]
    return flux


def stencil_kernel(levels, steps, n_edge, seat, cot, vw, zc, mc, smooth, halo, *rest):
    edges = rest[:n_edge]
    tail = edges[0].at[5] if n_edge == 1 else rest[n_edge]
    rest = rest[1:] if n_edge > 1 else rest
    edge_at = (1 - seat[0]) * (levels - 1)
    out, ready, final, wait, prior, spread, below_ref, sems, last_sem = rest[n_edge:]
    _, chunk, rows, _ = cot.shape
    tiles = rows // levels
    g = pl.program_id(0)
    slot = lax.rem(g, 2)
    lane = lax.broadcasted_iota(jnp.int32, (rows, 128), 1)
    row = lax.broadcasted_iota(jnp.int32, (rows, 128), 0)
    k = lax.rem(row, levels)
    cap_lane = lax.broadcasted_iota(jnp.int32, (2 * levels, 128), 1)
    cap_row = lax.broadcasted_iota(jnp.int32, (2 * levels, 128), 0)
    north = (cap_row < levels) & (cap_lane < POLAR)
    south = (cap_row >= levels) & (cap_lane >= 128 - POLAR)

    def first_copy():
        return pltpu.make_async_copy(
            ready.at[0, :, pl.ds(1, chunk - 1)], out.at[:, pl.ds(0, chunk - 1)], sems.at[0]
        )

    def copy(at):
        s = lax.rem(at, 2)
        return pltpu.make_async_copy(
            ready.at[s], out.at[:, pl.ds(at * chunk - 1, chunk)], sems.at[s]
        )

    @pl.when(g == 0)
    def _():
        spread[...] = jnp.zeros_like(spread)
        for f in range(5):
            prior[f] = halo[f, 0]
            wait[f] = jnp.zeros((rows, 128), jnp.float32)

    pl.when(g == 2)(lambda: first_copy().wait())
    pl.when(g > 2)(lambda: copy(g - 2).wait())

    def put(ref, at, value):
        if levels > 1:
            ref[pl.ds(at, tiles, stride=levels), :] = value
        else:
            ref[...] = value

    def one(l, _):
        for f in range(5):
            if n_edge == 1:
                put(spread.at[0, f], edge_at, edges[0][f, l])
            else:
                put(spread.at[0, f], levels - 1, edges[0][f, l])
                put(spread.at[1, f], 0, edges[1][f, l])
        for at in range(levels):
            put(below_ref, at, tail[l])
        wind = vw[l]
        base, fields = [], []
        for f in range(5):
            c = cot[f, l]
            w = wind * c
            a = c
            if levels > 1:
                up = jnp.where(k < levels - 1, pltpu.roll(w, rows - 1, 0), 0.0)
                a = a + (up - jnp.where(k > 0, pltpu.roll(w, 1, 0), 0.0))
            for n in range(n_edge):
                a = a + spread[n, f]
            if f == 3:
                theta = cot[2, l]
                below = below_ref[...] + theta
                for r in range(1, levels):
                    below = below + jnp.where(k < levels - r, pltpu.roll(theta, rows - r, 0), 0.0)
                a = a - COUPLE_B * below
            base.append(a)
            s = smooth[f, l]
            top = jnp.where(north, s, a[: 2 * levels])
            low = jnp.where(south, s, a[rows - 2 * levels :])
            fields.append(jnp.concatenate([top, a[2 * levels : rows - 2 * levels], low], 0))
        zonal = coupled(zc[l], fields, 0)
        merid = coupled(mc[l], fields, 1)
        for f in range(5):
            ready[slot, f, l] = wait[f] + zonal[f]
            left = pltpu.roll(merid[f], 1, 1)
            over = jnp.where(row < levels, 0.0, pltpu.roll(left, levels, 0))
            left = jnp.where(lane == 0, over, left)
            right = pltpu.roll(merid[f], 127, 1)
            over = jnp.where(row >= rows - levels, 0.0, pltpu.roll(right, rows - levels, 0))
            right = jnp.where(lane == 127, over, right)
            wait[f] = base[f] + (right - left) - prior[f]
            prior[f] = zonal[f]
        return 0

    lax.fori_loop(0, chunk, one, 0)
    pl.when(g == 0)(lambda: first_copy().start())
    pl.when(g > 0)(lambda: copy(g).start())

    @pl.when(g == steps - 1)
    def _():
        for f in range(5):
            final[f, 0] = wait[f] + halo[f, 1]
        end = pltpu.make_async_copy(final, out.at[:, pl.ds(steps * chunk - 1, 1)], last_sem)
        end.start()
        copy(g - 1).wait() if steps > 2 else first_copy().wait()
        copy(g).wait()
        end.wait()


def stencil(seat, cot, vw, zc, mc, smooth, halo, edges, levels):
    _, lon, rows, _ = cot.shape
    tiles = rows // levels
    chunk = chunk_of(lon)
    steps = lon // chunk
    field = lambda n: pl.BlockSpec((5, chunk, n, 128), lambda g, s: (0, g, 0, 0))
    plain = lambda n: pl.BlockSpec((chunk, n, 128), lambda g, s: (g, 0, 0))
    return pl.pallas_call(
        functools.partial(stencil_kernel, levels, steps, min(len(edges), 2)),
        out_shape=jax.ShapeDtypeStruct(cot.shape, jnp.float32),
        grid_spec=pltpu.PrefetchScalarGridSpec(
            num_scalar_prefetch=1,
            grid=(steps,),
            in_specs=[field(rows), plain(rows), plain(rows), plain(rows), field(2 * levels),
                      pl.BlockSpec((5, 2, rows, 128), lambda g, s: (0, 0, 0, 0))]
            + [pl.BlockSpec((6, chunk, tiles, 128), lambda g, s: (0, g, 0, 0))]
            if len(edges) == 1
            else [field(rows), plain(rows), plain(rows), plain(rows), field(2 * levels),
                  pl.BlockSpec((5, 2, rows, 128), lambda g, s: (0, 0, 0, 0)),
                  field(tiles), field(tiles), plain(tiles)],
            out_specs=pl.BlockSpec(memory_space=pl.ANY),
            scratch_shapes=[
                pltpu.VMEM((2, 5, chunk, rows, 128), jnp.float32),
                pltpu.VMEM((5, 1, rows, 128), jnp.float32),
                pltpu.VMEM((5, rows, 128), jnp.float32),
                pltpu.VMEM((5, rows, 128), jnp.float32),
                pltpu.VMEM((min(len(edges), 2), 5, rows, 128), jnp.float32),
                pltpu.VMEM((rows, 128), jnp.float32),
                pltpu.SemaphoreType.DMA((2,)),
                pltpu.SemaphoreType.DMA(()),
            ],
        ),
        compiler_params=pltpu.CompilerParams(vmem_limit_bytes=40 << 20),
        cost_estimate=pl.CostEstimate(
            flops=30 * 5 * lon * rows * 128, bytes_accessed=4 * 14 * lon * rows * 128, transcendentals=0
        ),
        name="stencil",
    )(seat, cot, vw, zc, mc, smooth, halo, *edges)


def swap_levels(first, last, total):
    count = lax.axis_size("lev")
    if count == 2:
        seat = lax.axis_index("lev")
        lead = jnp.concatenate([first, total[None]], 0)
        trail = jnp.concatenate([last, jnp.zeros_like(total)[None]], 0)
        got = lax.ppermute(jnp.where(seat == 0, trail, lead), "lev", [(0, 1), (1, 0)])
        return jnp.where(seat == 0, got[:5], 0.0), jnp.where(seat == 1, got[:5], 0.0), got[5]
    up = lax.ppermute(first, "lev", [(i + 1, i) for i in range(count - 1)])
    down = lax.ppermute(last, "lev", [(i, i + 1) for i in range(count - 1)])
    return up, down, later_sum(total)


def later_sum(local):
    count = lax.axis_size("lev")
    total = jnp.zeros_like(local)
    for r in range(1, count):
        total = total + lax.ppermute(local, "lev", [(i + r, i) for i in range(count - r)])
    return total


def ask_levels(cot, vw):
    return swap_levels(vw[0] * cot[:, 0], vw[-1] * cot[:, -1], cot[2].sum(0))


def adjoint_part(cot, vw, up, down, later):
    weighted = vw[None] * cot
    above = jnp.concatenate([weighted[:, 1:], up[:, None]], 1)
    under = jnp.concatenate([down[:, None], weighted[:, :-1]], 1)
    below = [later + cot[2, -1]]
    for k in range(cot.shape[1] - 2, -1, -1):
        below.insert(0, below[0] + cot[2, k])
    parts = cot + (above - under)
    return jnp.concatenate(
        [parts[:3], parts[3:4] - COUPLE_B * jnp.stack(below)[None], parts[4:]], 0
    )


def polar_cut(x):
    return jnp.concatenate([x[..., :POLAR], x[..., x.shape[-1] - POLAR :]], -1)


def body(cotangent, zonal_coef, merid_coef, vertical_wind, cutoff):
    levels, lon_dev, lat = cotangent.shape[1:]
    peers = lax.axis_size("lon")
    count = lax.axis_size("lev")
    seat = lax.axis_index("lev").astype(jnp.int32)[None]
    cot, vw = to_rows(cotangent), to_rows(vertical_wind)
    polar_cot = jnp.swapaxes(polar_cut(cotangent), 2, 3)
    polar_vw = jnp.swapaxes(polar_cut(vertical_wind), 1, 2)
    polar_got = ask_levels(polar_cot, polar_vw)
    ends_cot, ends_vw = cotangent[:, :, :: lon_dev - 1], vertical_wind[:, :: lon_dev - 1]
    ends_got = ask_levels(ends_cot, ends_vw)

    sends = edges_of(seat, cot, vw, levels, count == 2)
    polar_got, ends_got, sends = lax.optimization_barrier((polar_got, ends_got, sends))
    if count == 2:
        edges = [lax.ppermute(sends[0], "lev", [(0, 1), (1, 0)])]
    else:
        edges = [
            lax.ppermute(sends[0], "lev", [(i + 1, i) for i in range(count - 1)]),
            lax.ppermute(sends[1], "lev", [(i, i + 1) for i in range(count - 1)]),
            later_sum(sends[2]),
        ]
    polar = adjoint_part(polar_cot, polar_vw, *polar_got)
    ends_adj = adjoint_part(ends_cot, ends_vw, *ends_got)

    rows = 2 * POLAR // peers
    grouped = polar.reshape(5 * levels, peers, rows, lon_dev)
    grouped = jnp.swapaxes(grouped, 0, 1).reshape(peers, 5 * levels * rows, lon_dev)

    pack = jnp.concatenate([ends_adj.reshape(5 * levels, 2, lat), zonal_coef[:, :: lon_dev - 1]], 0)
    up = [(i, (i + 1) % peers) for i in range(peers)]
    down = [(j, i) for i, j in up]
    beyond = jnp.stack([lax.ppermute(pack[:, 1], "lon", up), lax.ppermute(pack[:, 0], "lon", down)], 1)
    halo_adj = beyond[: 5 * levels].reshape(5, levels, 2, lat)
    halo_zc = beyond[5 * levels :]

    smoothed = polar_filter(grouped, cutoff, peers)
    smoothed = smoothed.reshape(2, peers // 2, 5, levels, rows, lon_dev + 2)
    smoothed = smoothed.transpose(2, 5, 0, 3, 1, 4).reshape(5, lon_dev + 2, 2, levels, POLAR)
    north, south = smoothed[:, :, 0], smoothed[:, :, 1]
    gap = ((0, 0), (0, 0), (0, 0))
    smooth = jnp.concatenate(
        [jnp.pad(north, (*gap, (0, 128 - POLAR))), jnp.pad(south, (*gap, (128 - POLAR, 0)))], 2
    )[:, 1 : lon_dev + 1]
    outer = [jnp.swapaxes(x[:, :: lon_dev + 1], 1, 2) for x in (north, south)]
    halo_f = jnp.concatenate([outer[0], halo_adj[..., POLAR : lat - POLAR], outer[1]], 3)
    halo = jnp.stack(coupled(halo_zc, [halo_f[f] for f in range(5)], 0))
    out = stencil(
        seat, cot, vw, to_rows(zonal_coef), to_rows(merid_coef), smooth, to_rows(halo), edges, levels
    )
    return from_rows(out, levels)


def solution(mesh):
    return jax.shard_map(
        body,
        mesh=mesh,
        in_specs=(
            P(None, "lev", "lon", None),
            P("lev", "lon", None),
            P("lev", "lon", None),
            P("lev", "lon", None),
            P(),
        ),
        out_specs=P(None, "lev", "lon", None),
        check_vma=False,
    )
```
